128 devices in a mesh: grp: 8 (over y, z_hi), seq: 16 (over x, z_lo, core).
Axes of the slice: x: 4, y: 4, z: 4 (z_hi: 2, z_lo: 2; z = z_hi * 2 + z_lo), core: 2. Of those that a mesh axis runs over, the one named last changes fastest.
Arguments:
- queries: bfloat16 [8, 2048, 2048], P('grp', 'seq'), may hold values from -6 to 6
- keys: bfloat16 [8, 2048, 512], P('grp', 'seq'), may hold values from -6 to 6
- values: bfloat16 [8, 2048, 512], P('grp', 'seq'), may hold values from -6 to 6
- route_ids: int32 [8, 2048, 8], P('grp', 'seq'), may hold values from 0 to 127, all different within a row; in each aligned block of 128 rows (0 to 127, 128 to 255, ..., all dimensions but the last counted through in order) at most 9 rows name the same one
- route_weights: float32 [8, 2048, 8], P('grp', 'seq'), may hold values from 0.05 to 0.3
- out_weight: bfloat16 [2048, 2048], replicated, may hold values from -1.5909903 to 1.5909903
- norm_gain: float32 [2048], replicated, may hold values from 0.5 to 1.5
- gate_up: bfloat16 [128, 2048, 1536], P(('grp', 'seq')), may hold values from -0.125 to 0.125
- down_weight: bfloat16 [128, 768, 2048], P(('grp', 'seq')), may hold values from -0.21875 to 0.21875
Outputs:
- mixed: bfloat16 [8, 2048, 2048], P('grp', 'seq')
The draws below stay inside these ranges and needn't reach their ends.
Inputs may be any that keep to these rules, and one draw needn't show every extreme that they name: `route_ids`: each row names 8 different experts; the rows of one device name no expert more than 9 times, and in some devices' rows some expert exactly 9 times.
All inputs are finite; a program needn't handle non-finite values.
Results may differ from the reference program's by a relative error of at most 0.008.
Values may be sent and summed in bfloat16 or wider, within the bound.
No kernel may reach another device: no remote copies, remote signals or barrier semaphores. Data moves between devices by JAX's collectives and lax.ppermute only.
A program may use at most 128 MiB of HBM per device.

```python
import math
import jax
import jax.numpy as jnp
import numpy as np
from jax import lax

D = 2048
QUERY_HEADS = 16
KEY_VALUE_HEADS = 4
HEAD_WIDTH = 128
FF = 768
TOP = 8
TOK_DEV = 128
EXPERTS = 128
CAP = 9
SEQUENCE_COUNT = 8
TOKEN_LENGTH = 2048
N_GRP = 8
N_SEQ = 16


def draw_queries(key, part):
    input_source = jax.random.fold_in(key, 3)
    start_offset = jnp.clip(jax.random.normal(input_source, (SEQUENCE_COUNT, TOKEN_LENGTH, QUERY_HEADS, HEAD_WIDTH)), -6.0, 6.0)
    return start_offset.reshape(SEQUENCE_COUNT, TOKEN_LENGTH, QUERY_HEADS * HEAD_WIDTH).astype(jnp.bfloat16)


def draw_keys(key, part):
    input_source = jax.random.fold_in(key, 5)
    start_offset = jnp.clip(jax.random.normal(input_source, (SEQUENCE_COUNT, TOKEN_LENGTH, KEY_VALUE_HEADS, HEAD_WIDTH)), -6.0, 6.0)
    return start_offset.reshape(SEQUENCE_COUNT, TOKEN_LENGTH, KEY_VALUE_HEADS * HEAD_WIDTH).astype(jnp.bfloat16)


def draw_out_weight(key, part):
    first_operand, second_operand, third = jax.random.split(jax.random.fold_in(key, 9), 3)
    lower, upper = (0.5, 2.0)
    row_scale = jnp.exp(jax.random.uniform(second_operand, (QUERY_HEADS * HEAD_WIDTH, 1), minval=math.log(lower), maxval=math.log(upper)))
    col_scale = jnp.exp(jax.random.uniform(third, (1, D), minval=math.log(lower), maxval=math.log(upper)))
    start_offset = jnp.clip(jax.random.normal(first_operand, (QUERY_HEADS * HEAD_WIDTH, D)), -4.0, 4.0) * 2.0 / math.sqrt(QUERY_HEADS * HEAD_WIDTH)
    return (start_offset * row_scale * col_scale).astype(jnp.bfloat16)


def levels(key, extent, cuts, least, high):
    level = 1.0
    for dim, shards_of in cuts:
        draws = jax.random.uniform(jax.random.fold_in(jax.random.fold_in(key, 6), dim), (shards_of,), jnp.float32, least / len(cuts), high / len(cuts))
        level = level * jnp.repeat(jnp.exp(draws), extent[dim] // shards_of).reshape((-1,) + (1,) * (len(extent) - 1 - dim))
    return level


def shared_out(rng, own, number, rows, amount, top, limit, skew):
    order = jax.random.permutation(rng, amount)
    crowded, ordinary = load_shares(amount, rows * top, limit, skew, True), load_shares(amount, rows * top, limit, skew, False)
    places = jnp.arange(amount)

    def named(sizes, rotation):
        used = int((sizes > 0).sum())
        fixed = max(1, used // 4)
        shifted = fixed + (places - fixed + rotation * (used - fixed)) % max(1, amount - fixed)
        return jnp.zeros((amount,), jnp.int32).at[order[jnp.where(places < fixed, places, shifted)]].set(jnp.asarray(sizes, jnp.int32))

    sizes = jnp.where(number % 4 == 0, named(crowded, number // 4), named(ordinary, number - number // 4 - 1))
    mixed = jax.random.permutation(jax.random.fold_in(own, 3), amount)
    donor, sink = mixed[0:amount // 2 * 2:2], mixed[1:amount // 2 * 2:2]
    slack = jnp.minimum(sizes[donor] - 1, limit - sizes[sink]) // 2
    slack = jnp.where((donor == order[0]) | (sink == order[0]) | (sizes[sink] == 0), 0, jnp.maximum(slack, 0))
    shifted = jax.random.randint(jax.random.fold_in(own, 4), (amount // 2,), 0, 1 << 20) % (slack + 1)
    sizes = sizes.at[donor].add(-shifted).at[sink].add(shifted)
    items = jnp.searchsorted(jnp.cumsum(sizes), jnp.arange(rows * top), side="right").astype(jnp.int32)
    grid = items.reshape(top, rows).T
    grid = grid[jax.random.permutation(jax.random.fold_in(own, 1), rows)]
    rotation = jax.random.randint(jax.random.fold_in(own, 2), (rows, 1), 0, top)
    return jnp.take_along_axis(grid, (jnp.arange(top)[None, :] + rotation) % top, axis=1)


def load_shares(count, total, limit, lean, full):
    weights = [(1 << 20) // math.isqrt(rank ** lean) + 1 for rank in range(1, count + 1)]
    largest = limit if full else min(limit, max(-(-total // count), total * weights[0] // sum(weights)))
    least = 1 if total - largest >= count - 1 else 0
    given, rest = [largest] + [least] * (count - 1), total - largest - least * (count - 1)
    while rest > 0:
        free = [i for i in range(1, count) if given[i] < largest] or [i for i in range(1, count) if given[i] < limit]
        whole, remaining = sum([weights[i] for i in free]), rest
        for i in free:
            addition = min(limit - given[i], max(1, remaining * weights[i] // whole), rest)
            given[i] = given[i] + addition
            rest = rest - addition
    return np.array(given)


def bell_draw(stream_key, shape, scale, bound, cuts=(), held_as=jnp.bfloat16):
    loudness = levels(stream_key, shape, cuts, -0.22, 0.18) if cuts else 1.0
    drawn = jax.random.normal(stream_key, shape, jnp.float32) * scale * loudness
    return jnp.minimum(jnp.maximum(drawn, -bound), bound).astype(held_as)


def setup_inputs(seed: int = 0) -> dict:
    arg_keys = jax.random.split(jax.random.key(seed), 10)
    queries = draw_queries(jax.random.fold_in(arg_keys[9], 71), 0)
    keys = draw_keys(jax.random.fold_in(arg_keys[9], 71), 0)
    values = bell_draw(arg_keys[2], (SEQUENCE_COUNT, TOKEN_LENGTH, KEY_VALUE_HEADS * HEAD_WIDTH), 1.0, 6.0, ((0, 8), (1, 16)))
    route_ids_keys = jax.random.split(jax.random.fold_in(arg_keys[3], 1), SEQUENCE_COUNT * TOKEN_LENGTH // TOK_DEV)
    route_ids_turns = jax.random.permutation(jax.random.fold_in(arg_keys[3], 3), SEQUENCE_COUNT * TOKEN_LENGTH // TOK_DEV)
    route_ids = jax.vmap(lambda own, number: shared_out(jax.random.fold_in(arg_keys[3], 2), own, number, TOK_DEV, EXPERTS, TOP, CAP, 1))(route_ids_keys, route_ids_turns).reshape((SEQUENCE_COUNT, TOKEN_LENGTH, TOP))
    route_weights = jnp.clip(0.05 + 0.25 * jax.random.uniform(arg_keys[4], (SEQUENCE_COUNT, TOKEN_LENGTH, TOP), jnp.float32) ** levels(arg_keys[4], (SEQUENCE_COUNT, TOKEN_LENGTH, TOP), ((0, 8), (1, 16)), -0.2, 0.2), 0.05, 0.3)
    out_weight = draw_out_weight(jax.random.fold_in(arg_keys[9], 71), 0)
    norm_gain = jnp.clip(1.0 + 0.1 * jax.random.normal(arg_keys[6], (D,), jnp.float32), 0.5, 1.5)
    gate_up = bell_draw(arg_keys[7], (EXPERTS, D, 2 * FF), D ** -0.5, 0.125, ((0, 128),))
    down_weight = bell_draw(arg_keys[8], (EXPERTS, FF, D), FF ** -0.5, 0.21875, ((0, 128),))
    return {"queries": queries, "keys": keys, "values": values, "route_ids": route_ids, "route_weights": route_weights, "out_weight": out_weight, "norm_gain": norm_gain, "gate_up": gate_up, "down_weight": down_weight}


def normalize_rows(scores):
    highest = lax.optimization_barrier(jnp.max(scores, axis=-1, keepdims=True))
    raised = jnp.exp(scores - highest)
    return (raised / lax.optimization_barrier(jnp.sum(raised, axis=-1, keepdims=True))).astype(jnp.bfloat16)

def head_attention(packed):
    query, key_rows, value_rows = packed
    token_length = query.shape[0]
    scores = jnp.dot(query, key_rows.T, preferred_element_type=jnp.float32) * HEAD_WIDTH ** (-0.5)
    row_index = jnp.arange(token_length, dtype=jnp.int32)[:, None]
    col_index = jnp.arange(token_length, dtype=jnp.int32)[None, :]
    scores = jnp.where(col_index <= row_index, scores, -jnp.inf)
    return jnp.dot(normalize_rows(scores), value_rows, preferred_element_type=jnp.float32).astype(jnp.bfloat16)

def slot_numbers(block):
    onehot = (block[:, None] == jnp.arange(EXPERTS, dtype=jnp.int32)[None, :]).astype(jnp.int32)
    before = jnp.cumsum(onehot, axis=0) - onehot
    return lax.optimization_barrier(jnp.sum(before * onehot, axis=1)).astype(jnp.int32)

def reference(queries, keys, values, route_ids, route_weights, out_weight, norm_gain, gate_up, down_weight):
    sequence_total, token_length = (queries.shape[0], queries.shape[1])
    heads_per_group = QUERY_HEADS // KEY_VALUE_HEADS
    q_heads = queries.reshape(sequence_total, token_length, QUERY_HEADS, HEAD_WIDTH).transpose(0, 2, 1, 3).reshape(sequence_total * QUERY_HEADS, token_length, HEAD_WIDTH)
    key_heads = jnp.repeat(keys.reshape(sequence_total, token_length, KEY_VALUE_HEADS, HEAD_WIDTH).transpose(0, 2, 1, 3), heads_per_group, axis=1)
    key_heads = key_heads.reshape(sequence_total * QUERY_HEADS, token_length, HEAD_WIDTH)
    value_heads = jnp.repeat(values.reshape(sequence_total, token_length, KEY_VALUE_HEADS, HEAD_WIDTH).transpose(0, 2, 1, 3), heads_per_group, axis=1)
    value_heads = value_heads.reshape(sequence_total * QUERY_HEADS, token_length, HEAD_WIDTH)
    attended = lax.map(head_attention, (q_heads, key_heads, value_heads))
    attended = attended.reshape(sequence_total, QUERY_HEADS, token_length, HEAD_WIDTH).transpose(0, 2, 1, 3).reshape(sequence_total * token_length, QUERY_HEADS * HEAD_WIDTH)
    hidden_state = jnp.dot(attended, out_weight, preferred_element_type=jnp.float32)
    power = lax.optimization_barrier(jnp.mean(hidden_state * hidden_state, axis=-1, keepdims=True))
    normed = (hidden_state * lax.rsqrt(power + 1e-06) * norm_gain).astype(jnp.bfloat16)
    total = sequence_total * token_length
    devices = N_GRP * N_SEQ
    routes = TOK_DEV * TOP
    flat_ids = route_ids.reshape(devices, routes).astype(jnp.int32)
    slots = jax.vmap(slot_numbers)(flat_ids)
    target = flat_ids * CAP + slots
    owners = jnp.arange(devices, dtype=jnp.int32)[:, None] * TOK_DEV + jnp.arange(routes, dtype=jnp.int32)[None, :] // TOP
    row_select = jnp.broadcast_to(jnp.arange(devices, dtype=jnp.int32)[:, None], target.shape)
    table = jnp.full((devices, EXPERTS * CAP), total, jnp.int32).at[row_select, target].set(owners)
    shares = jnp.zeros((devices, EXPERTS * CAP), jnp.float32).at[row_select, target].set(route_weights.reshape(devices, routes).astype(jnp.float32))
    table = table.reshape(devices, EXPERTS, CAP).transpose(1, 0, 2).reshape(EXPERTS, devices * CAP)
    shares = shares.reshape(devices, EXPERTS, CAP).transpose(1, 0, 2).reshape(EXPERTS, devices * CAP)
    padded = jnp.concatenate([normed, jnp.zeros((1, D), jnp.bfloat16)], axis=0)

    def expert_step(summed, packed):
        table_row, share_row, gate_part, down_part = packed
        picked = padded[table_row]
        both = jnp.dot(picked, gate_part, preferred_element_type=jnp.float32)
        inner = (jax.nn.silu(both[:, :FF]) * both[:, FF:]).astype(jnp.bfloat16)
        result = jnp.dot(inner, down_part, preferred_element_type=jnp.float32).astype(jnp.bfloat16)
        return (summed.at[table_row].add(result.astype(jnp.float32) * share_row[:, None]), None)
    summed, _ = lax.scan(expert_step, jnp.zeros((total + 1, D), jnp.float32), (table, shares, gate_up, down_weight))
    return (hidden_state + summed[:total]).astype(jnp.bfloat16).reshape(sequence_total, token_length, D)
```

```python
import functools

import jax
import jax.numpy as jnp
from jax import lax
from jax.experimental import pallas as pl
from jax.experimental.pallas import tpu as pltpu
from jax.sharding import PartitionSpec as P

BF16, F32 = jnp.bfloat16, jnp.float32
D = 2048
HEAD = 128
FF = 768
TOP = 8
ROWS = 8
FOLD = D // ROWS
WIDE = D + FOLD
EXPERTS = 128
TOK = 128
VMEM = pl.BlockSpec(memory_space=pltpu.VMEM)


def dot(a, b, dims=((1,), (0,))):
    return lax.dot_general(a, b, (dims, ((), ())), preferred_element_type=F32)


def iota(shape, dim):
    return lax.broadcasted_iota(jnp.int32, shape, dim)


def call(kernel, out, scratch=(), limit=None):
    return pl.pallas_call(
        kernel,
        out_shape=out,
        scratch_shapes=scratch,
        compiler_params=pltpu.CompilerParams(vmem_limit_bytes=limit),
    )


def pack_kernel(heads, shared, q_ref, k_ref, v_ref, o_ref):
    rows = q_ref.shape[0]
    for h in range(heads):
        g = h // shared
        at = h * 3 * rows
        o_ref[at : at + rows, :] = q_ref[:, h * HEAD : (h + 1) * HEAD]
        o_ref[at + rows : at + 2 * rows, :] = k_ref[:, g * HEAD : (g + 1) * HEAD]
        o_ref[at + 2 * rows : at + 3 * rows, :] = v_ref[:, g * HEAD : (g + 1) * HEAD]


def attention_kernel(blocks, rows, x_ref, o_ref, k_s, v_s):
    for s in range(blocks):
        at = s * 3 * rows
        k_s[s * rows : (s + 1) * rows, :] = x_ref[at + rows : at + 2 * rows, :]
        v_s[s * rows : (s + 1) * rows, :] = x_ref[at + 2 * rows : at + 3 * rows, :]
    factor = HEAD ** (-0.5) * 1.4426950408889634
    two = 2 * rows
    keep = iota((two, two), 1) <= iota((two, two), 0)
    for i in range(blocks // 2):
        at = 2 * i * 3 * rows
        q = jnp.concatenate([x_ref[at : at + rows, :], x_ref[at + 3 * rows : at + 4 * rows, :]], axis=0)
        own = dot(q, k_s[i * two : (i + 1) * two, :], ((1,), (1,)))
        own = jnp.where(keep, own, -jnp.inf)
        top = jnp.max(own, axis=-1, keepdims=True)
        if i:
            past = dot(q, k_s[: i * two, :], ((1,), (1,)))
            top = jnp.maximum(top, jnp.max(past, axis=-1, keepdims=True))
            past = jnp.exp2((past - top) * factor)
        own = jnp.exp2((own - top) * factor)
        total = jnp.sum(own, axis=-1, keepdims=True)
        if i:
            total += jnp.sum(past, axis=-1, keepdims=True)
        share = 1.0 / total
        out = dot((own * share).astype(BF16), v_s[i * two : (i + 1) * two, :])
        if i:
            out += dot((past * share).astype(BF16), v_s[: i * two, :])
        o_ref[i * two : (i + 1) * two, :] = out.astype(BF16)


def places(ids):
    named = jnp.zeros((TOK, EXPERTS), F32)
    lanes = iota((TOK, EXPERTS), 1)
    for j in range(TOP):
        named += jnp.where(ids[:, j : j + 1] == lanes, 1.0, 0.0)
    named = named.T
    before = jnp.where(iota((TOK, TOK), 0) < iota((TOK, TOK), 1), 1.0, 0.0).astype(BF16)
    slot = dot(named.astype(BF16), before)
    return jnp.where(named > 0.5, slot, -1.0)


def spread(rows):
    n, t = rows.shape
    return jnp.broadcast_to(rows[:, None, :], (n, ROWS, t)).reshape(n * ROWS, t)


def folded(piece, count):
    shape = (count, ROWS * count)
    return jnp.where(iota(shape, 1) == iota(shape, 0) * ROWS + piece, 1.0, 0.0).astype(BF16)


def unfolded(piece, count):
    shape = (ROWS * count, count)
    return jnp.where(iota(shape, 0) == iota(shape, 1) * ROWS + piece, 1.0, 0.0).astype(BF16)


def project_kernel(heads, a_ref, w_ref, gain_ref, ids_ref, hidden_ref, o_ref, normed_s):
    rows = TOK
    a = jnp.concatenate([a_ref[h * rows : (h + 1) * rows, :] for h in range(heads)], axis=1)
    power = jnp.zeros((rows, 1), F32)
    step = 512
    for c in range(0, D, step):
        h = dot(a, w_ref[:, c : c + step])
        hidden_ref[:, c : c + step] = h
        power += jnp.sum(h * h, axis=-1, keepdims=True)
    scale = lax.rsqrt(power * (1.0 / D) + 1e-06)
    for c in range(0, D, step):
        normed_s[:, c : c + step] = (
            hidden_ref[:, c : c + step] * scale * gain_ref[:, c : c + step]
        ).astype(BF16)
    place = places(ids_ref[...])
    wide = spread(place)
    which = iota((EXPERTS * ROWS, TOK), 0) % ROWS
    pick = jnp.where(wide == which.astype(F32), 1.0, 0.0).astype(BF16)
    last = jnp.zeros((EXPERTS * ROWS, FOLD), F32)
    for c in range(ROWS):
        piece = normed_s[:, c * FOLD : (c + 1) * FOLD]
        o_ref[:, c * FOLD : (c + 1) * FOLD] = dot(pick, piece).astype(BF16)
        ninth = jnp.where((wide == float(ROWS)) & (which == c), 1.0, 0.0).astype(BF16)
        last += dot(ninth, piece)
    o_ref[:, D:] = last.astype(BF16)


def expert_kernel(count, x_ref, wide_ref, down_ref, o_ref, last_s, result_s):
    def mlp(x):
        gate = dot(x, wide_ref[:, :FF])
        up = dot(x, wide_ref[:, FF:])
        inner = (gate / (1.0 + jnp.exp(-gate)) * up).astype(BF16)
        return dot(inner, down_ref[...]).astype(BF16)

    block = 256

    def step(b, carry):
        at = pl.multiple_of(b * block, block)
        o_ref[pl.ds(at, block), :D] = mlp(x_ref[pl.ds(at, block), :D])
        return carry

    lax.fori_loop(0, count * ROWS // block, step, 0)
    tail = x_ref[:, D:]
    for c in range(ROWS):
        last_s[:, c * FOLD : (c + 1) * FOLD] = dot(folded(c, count), tail).astype(BF16)
    result_s[...] = mlp(last_s[...])
    back = jnp.zeros((count * ROWS, FOLD), F32)
    for c in range(ROWS):
        back += dot(unfolded(c, count), result_s[:, c * FOLD : (c + 1) * FOLD])
    o_ref[:, D:] = back.astype(BF16)


def combine_kernel(y_ref, hidden_ref, ids_ref, weights_ref, o_ref):
    ids = ids_ref[...]
    place = places(ids)
    weight = jnp.zeros((TOK, EXPERTS), F32)
    lanes = iota((TOK, EXPERTS), 1)
    for j in range(TOP):
        weight += jnp.where(ids[:, j : j + 1] == lanes, weights_ref[:, j : j + 1], 0.0)
    weight = weight.T
    which = (iota((EXPERTS * ROWS, TOK), 0) % ROWS).astype(F32)
    share = jnp.where(spread(place) == which, spread(weight), 0.0)
    ninth = jnp.where(place == float(ROWS), weight, 0.0)

    def halves(value):
        high = value.astype(BF16)
        return high, (value - high.astype(F32)).astype(BF16)

    share_high, share_low = halves(share.T)
    ninth_high, ninth_low = halves(ninth.T)
    tail = y_ref[:, D:]
    for c in range(ROWS):
        cols = slice(c * FOLD, (c + 1) * FOLD)
        y = y_ref[:, cols]
        last = dot(folded(c, EXPERTS), tail).astype(BF16)
        mixture = dot(share_high, y) + dot(share_low, y) + dot(ninth_high, last) + dot(ninth_low, last)
        o_ref[:, cols] = (hidden_ref[:, cols] + mixture).astype(BF16)


def exchange(value, axes):
    return lax.all_to_all(value, axes, split_axis=0, concat_axis=0, tiled=True)


def shaped(*dims, dtype=BF16):
    return jax.ShapeDtypeStruct(dims, dtype)


def on_device(
    queries, keys, values, route_ids, route_weights, out_weight, norm_gain, gate_up, down_weight
):
    heads, groups = queries.shape[2] // HEAD, keys.shape[2] // HEAD
    blocks = lax.axis_size("seq")
    ids = route_ids[0]
    packed = call(
        functools.partial(pack_kernel, heads, heads // groups), shaped(heads * 3 * TOK, HEAD)
    )(queries[0], keys[0], values[0])
    packed = exchange(packed, "seq")
    attended = call(
        functools.partial(attention_kernel, blocks, TOK),
        shaped(blocks * TOK, HEAD),
        [pltpu.VMEM((blocks * TOK, HEAD), BF16)] * 2,
    )(packed)
    attended = exchange(attended, "seq")
    hidden, outgoing = call(
        functools.partial(project_kernel, heads),
        (shaped(TOK, D, dtype=F32), shaped(EXPERTS * ROWS, WIDE)),
        [pltpu.VMEM((TOK, D), BF16)],
    )(attended, out_weight, norm_gain[None], ids)
    arrived = exchange(outgoing, ("grp", "seq"))
    result = call(
        functools.partial(expert_kernel, EXPERTS),
        shaped(EXPERTS * ROWS, WIDE),
        [pltpu.VMEM((EXPERTS, D), BF16), pltpu.VMEM((EXPERTS, D), BF16)],
    )(arrived, gate_up[0], down_weight[0])
    returned = exchange(result, ("grp", "seq"))
    mixed = call(combine_kernel, shaped(TOK, D))(returned, hidden, ids, route_weights[0])
    return mixed[None]


def solution(mesh):
    placed = (
        P("grp", "seq", None),
        P("grp", "seq", None),
        P("grp", "seq", None),
        P("grp", "seq", None),
        P("grp", "seq", None),
        P(),
        P(),
        P(("grp", "seq"), None, None),
        P(("grp", "seq"), None, None),
    )
    return jax.shard_map(
        on_device, mesh=mesh, in_specs=placed, out_specs=P("grp", "seq", None), check_vma=False
    )
```

```python
import functools

import jax
import jax.numpy as jnp
from jax import lax
from jax.experimental import pallas as pl
from jax.experimental.pallas import tpu as pltpu
from jax.sharding import PartitionSpec as P


BF16, F32 = jnp.bfloat16, jnp.float32
D = 2048
HEAD = 128
FF = 768
TOP = 8
ROWS = 8
FOLD = D // ROWS
WIDE = D + FOLD
EXPERTS = 128
TOK = 128
VMEM = pl.BlockSpec(memory_space=pltpu.VMEM)


def dot(a, b, dims=((1,), (0,))):
    return lax.dot_general(a, b, (dims, ((), ())), preferred_element_type=F32)


def iota(shape, dim):
    return lax.broadcasted_iota(jnp.int32, shape, dim)


def call(kernel, out, scratch=(), limit=20 << 20, cost=None, **spec):
    return pl.pallas_call(
        kernel,
        out_shape=out,
        scratch_shapes=scratch,
        compiler_params=pltpu.CompilerParams(vmem_limit_bytes=limit),
        cost_estimate=cost,
        **spec,
    )


def pack_kernel(parts, shared, q_far, k_far, v_far, *refs):
    outs, (q_ref, k_ref, v_ref, sems) = refs[: 2 * parts], refs[2 * parts :]
    loads = [
        pltpu.make_async_copy(far, near, sems.at[n])
        for n, (far, near) in enumerate(((k_far, k_ref), (v_far, v_ref), (q_far, q_ref)))
    ]
    for load in loads:
        load.start()
    mine = lax.axis_index("seq") // parts
    for load in loads:
        load.wait()
    for s in range(parts):
        g = lax.rem(mine + s, parts)
        kv_ref, query_ref = outs[s], outs[parts + s]
        lane = pl.multiple_of(g * HEAD, HEAD)
        kv_ref[:TOK, :] = k_ref[:, pl.ds(lane, HEAD)]
        kv_ref[TOK:, :] = v_ref[:, pl.ds(lane, HEAD)]
        for h in range(shared):
            lane = pl.multiple_of(g * (shared * HEAD), HEAD) + h * HEAD
            query_ref[h * TOK : (h + 1) * TOK, :] = q_ref[:, pl.ds(lane, HEAD)]


def join_kernel(parts, *refs):
    mine = lax.axis_index("seq") // parts
    for s in range(parts):
        at = pl.multiple_of(lax.rem(mine - s + parts, parts) * (2 * TOK), 2 * TOK)
        refs[parts][pl.ds(at, 2 * TOK), :] = refs[s][...]


def attention_kernel(parts, shared, *refs):
    kvs, queries, w_ref = refs[:4], refs[4 : 4 + parts], refs[4 + parts]
    outs, near_ref = refs[5 + parts : 5 + 2 * parts], refs[5 + 2 * parts]
    k_s, v_s, q_s, o_s, sem = refs[6 + 2 * parts :]
    carry = pltpu.make_async_copy(w_ref, near_ref, sem)
    carry.start()
    me = lax.axis_index("seq")
    mine, lane_id = me // parts, lax.rem(me, parts)
    rows, keys = shared * TOK, 4 * TOK
    for d in range(4):
        for p in range(parts):
            at = pl.multiple_of((p * 4 + (lane_id ^ d)) * TOK, TOK)
            k_s[pl.ds(at, TOK), :] = kvs[d][p * 2 * TOK : (p * 2 + 1) * TOK, :]
            v_s[pl.ds(at, TOK), :] = kvs[d][(p * 2 + 1) * TOK : (p * 2 + 2) * TOK, :]
    for s in range(parts):
        at = pl.multiple_of(lax.rem(mine - s + parts, parts) * rows, rows)
        q_s[pl.ds(at, rows), :] = queries[s][...]
    factor = HEAD ** (-0.5) * 1.4426950408889634
    keep = iota((rows, keys), 1) <= iota((rows, keys), 0) % TOK + lane_id * TOK
    for i in range(parts):
        q = q_s[i * rows : (i + 1) * rows, :]
        own = dot(q, k_s[i * keys : (i + 1) * keys, :], ((1,), (1,)))
        own = jnp.where(keep, own, -jnp.inf)
        top = jnp.max(own, axis=-1, keepdims=True)
        if i:
            past = dot(q, k_s[: i * keys, :], ((1,), (1,)))
            top = jnp.maximum(top, jnp.max(past, axis=-1, keepdims=True))
            past = jnp.exp2((past - top) * factor)
        own = jnp.exp2((own - top) * factor)
        total = jnp.sum(own, axis=-1, keepdims=True)
        if i:
            total += jnp.sum(past, axis=-1, keepdims=True)
        share = 1.0 / total
        out = dot((own * share).astype(BF16), v_s[i * keys : (i + 1) * keys, :])
        if i:
            out += dot((past * share).astype(BF16), v_s[: i * keys, :])
        o_s[i * rows : (i + 1) * rows, :] = out.astype(BF16)
    for s in range(parts):
        at = pl.multiple_of(lax.rem(mine + s, parts) * rows, rows)
        outs[s][...] = o_s[pl.ds(at, rows), :]
    carry.wait()


def named(ids):
    experts = iota((EXPERTS, TOK), 0)
    return [ids[j : j + 1, :] == experts for j in range(TOP)]


def places(ids):
    hit = jnp.zeros((EXPERTS, TOK), F32)
    for match in named(ids):
        hit += jnp.where(match, 1.0, 0.0)
    before = jnp.where(iota((TOK, TOK), 0) < iota((TOK, TOK), 1), 1.0, 0.0).astype(BF16)
    return jnp.where(hit > 0.5, dot(hit.astype(BF16), before), -1.0)


def spread(rows):
    n, t = rows.shape
    return jnp.broadcast_to(rows[:, None, :], (n, ROWS, t)).reshape(n * ROWS, t)


def put_fold(fold_s, c, value):
    for half in range(FOLD // HEAD):
        fold_s[half, pl.ds(c, value.shape[0], stride=ROWS), :] = value[:, half * HEAD : (half + 1) * HEAD]


def take_fold(fold_s, c, count):
    halves = [fold_s[half, pl.ds(c, count, stride=ROWS), :] for half in range(FOLD // HEAD)]
    return jnp.concatenate(halves, axis=1).astype(BF16)


def load_fold(fold_s, tail):
    for half in range(FOLD // HEAD):
        fold_s[half] = tail[:, half * HEAD : (half + 1) * HEAD].astype(F32)


def whole_fold(fold_s):
    return jnp.concatenate([fold_s[half] for half in range(FOLD // HEAD)], axis=1).astype(BF16)


def project_kernel(parts, shared, *refs):
    pieces = refs[:parts]
    w_ref, gain_ref, ids_ref, hidden_ref, o_ref, normed_s, fold_s = refs[parts:]
    mine = lax.axis_index("seq") // parts
    wide, rows = shared * HEAD, TOK
    power = jnp.zeros((rows, 1), F32)
    step = 512
    for c in range(0, D, step):
        h = jnp.zeros((rows, step), F32)
        for s in range(parts):
            a = jnp.concatenate([pieces[s][g * rows : (g + 1) * rows, :] for g in range(shared)], axis=1)
            at = pl.multiple_of(lax.rem(mine - s + parts, parts) * wide, wide)
            h += dot(a, w_ref[pl.ds(at, wide), c : c + step])
        hidden_ref[:, c : c + step] = h
        power += jnp.sum(h * h, axis=-1, keepdims=True)
    scale = lax.rsqrt(power * (1.0 / D) + 1e-06)
    for c in range(0, D, step):
        normed_s[:, c : c + step] = (
            hidden_ref[:, c : c + step] * scale * gain_ref[:, c : c + step]
        ).astype(BF16)
    place = places(ids_ref[...])
    wide = spread(place)
    which = iota((EXPERTS * ROWS, TOK), 0) % ROWS
    pick = jnp.where(wide == which.astype(F32), 1.0, 0.0).astype(BF16)
    ninth = jnp.where(place == float(ROWS), 1.0, 0.0).astype(BF16)
    for c in range(ROWS):
        piece = normed_s[:, c * FOLD : (c + 1) * FOLD]
        o_ref[:, c * FOLD : (c + 1) * FOLD] = dot(pick, piece).astype(BF16)
        put_fold(fold_s, c, dot(ninth, piece))
    o_ref[:, D:] = whole_fold(fold_s)


def expert_kernel(count, x_ref, wide_ref, down_ref, o_ref, last_s, fold_s):
    def mlp(x):
        gate = dot(x, wide_ref[:, :FF])
        up = dot(x, wide_ref[:, FF:])
        inner = (gate / (1.0 + jnp.exp(-gate)) * up).astype(BF16)
        return dot(inner, down_ref[...])

    block = 256
    for b in range(0, count * ROWS, block):
        o_ref[b : b + block, :D] = mlp(x_ref[b : b + block, :D]).astype(BF16)
    load_fold(fold_s, x_ref[:, D:])
    for c in range(ROWS):
        last_s[:, c * FOLD : (c + 1) * FOLD] = take_fold(fold_s, c, count)
    last = mlp(last_s[...])
    for c in range(ROWS):
        put_fold(fold_s, c, last[:, c * FOLD : (c + 1) * FOLD])
    o_ref[:, D:] = whole_fold(fold_s)


def share_kernel(ids_ref, weights_ref, share_ref, ninth_ref):
    def halves(value, ref):
        high = value.astype(BF16)
        ref[:TOK, :] = high
        ref[TOK:, :] = (value - high.astype(F32)).astype(BF16)

    ids = ids_ref[...]
    place = places(ids)
    weight = jnp.zeros((EXPERTS, TOK), F32)
    for j, match in enumerate(named(ids)):
        weight += jnp.where(match, weights_ref[j : j + 1, :], 0.0)
    which = (iota((EXPERTS * ROWS, TOK), 0) % ROWS).astype(F32)
    halves(jnp.where(spread(place) == which, spread(weight), 0.0).T, share_ref)
    halves(jnp.where(place == float(ROWS), weight, 0.0).T, ninth_ref)


def combine_kernel(y_ref, share_ref, ninth_ref, hidden_ref, o_ref, fold_s):
    load_fold(fold_s, y_ref[:, D:])
    for c in range(ROWS):
        cols = slice(c * FOLD, (c + 1) * FOLD)
        last = take_fold(fold_s, c, EXPERTS)
        mixture = dot(share_ref[...], y_ref[:, cols]) + dot(ninth_ref[...], last)
        o_ref[:, cols] = (hidden_ref[:, cols] + mixture[:TOK] + mixture[TOK:]).astype(BF16)


def exchange(value, axes):
    return lax.all_to_all(value, axes, split_axis=0, concat_axis=0, tiled=True)


def shaped(*dims, dtype=BF16):
    return jax.ShapeDtypeStruct(dims, dtype)


def on_device(
    queries, keys, values, route_ids, route_weights, out_weight, norm_gain, gate_up, down_weight
):
    heads, parts = queries.shape[2] // HEAD, keys.shape[2] // HEAD
    shared = heads // parts
    size = lax.axis_size("seq")
    ids = route_ids[0].T

    def ahead(value, s):
        return lax.ppermute(value, "seq", [(i, (i + s * parts) % size) for i in range(size)])

    def across(value, d):
        return lax.ppermute(value, "seq", [(i, i ^ d) for i in range(size)])

    kv, query = shaped(2 * TOK, HEAD), shaped(shared * TOK, HEAD)
    sent = call(
        functools.partial(pack_kernel, parts, shared),
        (kv,) * parts + (query,) * parts,
        [pltpu.VMEM(a.shape[1:], BF16) for a in (queries, keys, values)] + [pltpu.SemaphoreType.DMA((3,))],
        limit=107 << 19,
        in_specs=[pl.BlockSpec(memory_space=pltpu.HBM)] * 3,
    )(queries[0], keys[0], values[0])
    kvs = [sent[0]] + [ahead(sent[s], s) for s in range(1, parts)]
    asked = [sent[parts]] + [ahead(sent[parts + s], s) for s in range(1, parts)]
    line = call(functools.partial(join_kernel, parts), shaped(parts * 2 * TOK, HEAD))(*kvs)
    flipped = across(line, 2)
    gathered = [line, across(line, 1), flipped, across(flipped, 1)]
    share, ninth = call(
        share_kernel, (shaped(2 * TOK, EXPERTS * ROWS), shaped(2 * TOK, EXPERTS))
    )(ids, route_weights[0].T)
    gathered, share, ninth = lax.optimization_barrier((gathered, share, ninth))
    *attended, weight = call(
        functools.partial(attention_kernel, parts, shared),
        (query,) * parts + (shaped(*out_weight.shape),),
        [pltpu.VMEM((size * TOK, HEAD), BF16)] * 2
        + [pltpu.VMEM((parts * shared * TOK, HEAD), BF16)] * 2
        + [pltpu.SemaphoreType.DMA],
        limit=40 << 20,
        in_specs=[VMEM] * (4 + parts) + [pl.BlockSpec(memory_space=pltpu.HBM)],
        out_specs=(VMEM,) * (parts + 1),
    )(*gathered, *asked, out_weight)
    attended = [attended[0]] + [ahead(attended[s], s) for s in range(1, parts)]
    hidden, outgoing = call(
        functools.partial(project_kernel, parts, shared),
        (shaped(TOK, D, dtype=F32), shaped(EXPERTS * ROWS, WIDE)),
        [pltpu.VMEM((TOK, D), BF16), pltpu.VMEM((FOLD // HEAD, EXPERTS * ROWS, HEAD), F32)],
    )(*attended, weight, norm_gain[None], ids)
    arrived = exchange(outgoing, ("grp", "seq"))
    fold = pltpu.VMEM((FOLD // HEAD, EXPERTS * ROWS, HEAD), F32)
    result = call(
        functools.partial(expert_kernel, EXPERTS),
        shaped(EXPERTS * ROWS, WIDE),
        [pltpu.VMEM((EXPERTS, D), BF16), fold],
    )(arrived, gate_up[0], down_weight[0])
    returned = exchange(result, ("grp", "seq"))
    mixed = call(combine_kernel, shaped(TOK, D), [fold])(returned, share, ninth, hidden)
    return mixed[None]


def solution(mesh):
    placed = (
        P("grp", "seq", None),
        P("grp", "seq", None),
        P("grp", "seq", None),
        P("grp", "seq", None),
        P("grp", "seq", None),
        P(),
        P(),
        P(("grp", "seq"), None, None),
        P(("grp", "seq"), None, None),
    )

    return jax.shard_map(on_device, mesh=mesh, in_specs=placed, out_specs=P("grp", "seq", None), check_vma=False)
```

```python
import functools

import jax
import jax.numpy as jnp
from jax import lax
from jax.experimental import pallas as pl
from jax.experimental.pallas import tpu as pltpu
from jax.sharding import PartitionSpec as P


BF16, F32 = jnp.bfloat16, jnp.float32
D = 2048
HEAD = 128
FF = 768
TOP = 8
ROWS = 8
FOLD = D // ROWS
WIDE = D + FOLD
EXPERTS = 128
TOK = 128
VMEM = pl.BlockSpec(memory_space=pltpu.VMEM)


def dot(a, b, dims=((1,), (0,))):
    return lax.dot_general(a, b, (dims, ((), ())), preferred_element_type=F32)


def iota(shape, dim):
    return lax.broadcasted_iota(jnp.int32, shape, dim)


def call(kernel, out, scratch=(), limit=20 << 20, cost=None, **spec):
    return pl.pallas_call(
        kernel,
        out_shape=out,
        scratch_shapes=scratch,
        compiler_params=pltpu.CompilerParams(vmem_limit_bytes=limit),
        cost_estimate=cost,
        **spec,
    )


def pack_kernel(parts, shared, q_far, k_far, v_far, *refs):
    outs, (q_ref, k_ref, v_ref, sems) = refs[: 2 * parts], refs[2 * parts :]
    loads = [
        pltpu.make_async_copy(far, near, sems.at[n])
        for n, (far, near) in enumerate(((k_far, k_ref), (v_far, v_ref), (q_far, q_ref)))
    ]
    for load in loads:
        load.start()
    mine = lax.axis_index("seq") // parts
    for load in loads:
        load.wait()
    for s in range(parts):
        g = lax.rem(mine + s, parts)
        kv_ref, query_ref = outs[s], outs[parts + s]
        lane = pl.multiple_of(g * HEAD, HEAD)
        kv_ref[:TOK, :] = k_ref[:, pl.ds(lane, HEAD)]
        kv_ref[TOK:, :] = v_ref[:, pl.ds(lane, HEAD)]
        for h in range(shared):
            lane = pl.multiple_of(g * (shared * HEAD), HEAD) + h * HEAD
            query_ref[h * TOK : (h + 1) * TOK, :] = q_ref[:, pl.ds(lane, HEAD)]


def join_kernel(parts, *refs):
    mine = lax.axis_index("seq") // parts
    for s in range(parts):
        at = pl.multiple_of(lax.rem(mine - s + parts, parts) * (2 * TOK), 2 * TOK)
        refs[parts][pl.ds(at, 2 * TOK), :] = refs[s][...]


def attention_kernel(parts, shared, *refs):
    kvs, queries, w_ref = refs[:4], refs[4 : 4 + parts], refs[4 + parts]
    outs, near_ref = refs[5 + parts : 5 + 2 * parts], refs[5 + 2 * parts]
    k_s, v_s, q_s, o_s, sem = refs[6 + 2 * parts :]
    carry = pltpu.make_async_copy(w_ref, near_ref, sem)
    carry.start()
    me = lax.axis_index("seq")
    mine, lane_id = me // parts, lax.rem(me, parts)
    rows, keys = shared * TOK, 4 * TOK
    for d in range(4):
        for p in range(parts):
            at = pl.multiple_of((p * 4 + (lane_id ^ d)) * TOK, TOK)
            k_s[pl.ds(at, TOK), :] = kvs[d][p * 2 * TOK : (p * 2 + 1) * TOK, :]
            v_s[pl.ds(at, TOK), :] = kvs[d][(p * 2 + 1) * TOK : (p * 2 + 2) * TOK, :]
    for s in range(parts):
        at = pl.multiple_of(lax.rem(mine - s + parts, parts) * rows, rows)
        q_s[pl.ds(at, rows), :] = queries[s][...]
    factor = HEAD ** (-0.5) * 1.4426950408889634
    keep = iota((rows, keys), 1) <= iota((rows, keys), 0) % TOK + lane_id * TOK
    for i in range(parts):
        q = q_s[i * rows : (i + 1) * rows, :]
        own = dot(q, k_s[i * keys : (i + 1) * keys, :], ((1,), (1,)))
        own = jnp.where(keep, own, -jnp.inf)
        top = jnp.max(own, axis=-1, keepdims=True)
        if i:
            past = dot(q, k_s[: i * keys, :], ((1,), (1,)))
            top = jnp.maximum(top, jnp.max(past, axis=-1, keepdims=True))
            past = jnp.exp2((past - top) * factor)
        own = jnp.exp2((own - top) * factor)
        total = jnp.sum(own, axis=-1, keepdims=True)
        if i:
            total += jnp.sum(past, axis=-1, keepdims=True)
        share = 1.0 / total
        out = dot((own * share).astype(BF16), v_s[i * keys : (i + 1) * keys, :])
        if i:
            out += dot((past * share).astype(BF16), v_s[: i * keys, :])
        o_s[i * rows : (i + 1) * rows, :] = out.astype(BF16)
    for s in range(parts):
        at = pl.multiple_of(lax.rem(mine + s, parts) * rows, rows)
        outs[s][...] = o_s[pl.ds(at, rows), :]
    carry.wait()


def named(ids):
    experts = iota((EXPERTS, TOK), 0)
    return [ids[j : j + 1, :] == experts for j in range(TOP)]


def places(ids):
    hit = jnp.zeros((EXPERTS, TOK), F32)
    for match in named(ids):
        hit += jnp.where(match, 1.0, 0.0)
    before = jnp.where(iota((TOK, TOK), 0) < iota((TOK, TOK), 1), 1.0, 0.0).astype(BF16)
    return jnp.where(hit > 0.5, dot(hit.astype(BF16), before), -1.0)


def spread(rows):
    n, t = rows.shape
    return jnp.broadcast_to(rows[:, None, :], (n, ROWS, t)).reshape(n * ROWS, t)


def put_fold(fold_s, c, value):
    for half in range(FOLD // HEAD):
        fold_s[half, pl.ds(c, value.shape[0], stride=ROWS), :] = value[:, half * HEAD : (half + 1) * HEAD]


def take_fold(fold_s, c, count):
    halves = [fold_s[half, pl.ds(c, count, stride=ROWS), :] for half in range(FOLD // HEAD)]
    return jnp.concatenate(halves, axis=1).astype(BF16)


def load_fold(fold_s, tail):
    for half in range(FOLD // HEAD):
        fold_s[half] = tail[:, half * HEAD : (half + 1) * HEAD].astype(F32)


def whole_fold(fold_s):
    return jnp.concatenate([fold_s[half] for half in range(FOLD // HEAD)], axis=1).astype(BF16)


def head_rows(piece, shared):
    return jnp.concatenate([piece[g * TOK : (g + 1) * TOK, :] for g in range(shared)], axis=1)


def weight_rows(parts, shared, s):
    mine = lax.axis_index("seq") // parts
    wide = shared * HEAD
    return pl.ds(pl.multiple_of(lax.rem(mine - s + parts, parts) * wide, wide), wide)


def prepare_kernel(
    parts, shared, a_ref, w_ref, ids_ref, weights_ref, part_ref, pick_ref, nine_ref, share_ref, ninth_ref
):
    a = head_rows(a_ref, shared)
    rows = weight_rows(parts, shared, 0)
    for c in range(0, D, 512):
        part_ref[:, c : c + 512] = dot(a, w_ref[rows, c : c + 512])

    def halves(value, ref):
        high = value.astype(BF16)
        ref[:TOK, :] = high
        ref[TOK:, :] = (value - high.astype(F32)).astype(BF16)

    ids = ids_ref[...]
    place = places(ids)
    weight = jnp.zeros((EXPERTS, TOK), F32)
    for j, match in enumerate(named(ids)):
        weight += jnp.where(match, weights_ref[j : j + 1, :], 0.0)
    which = (iota((EXPERTS * ROWS, TOK), 0) % ROWS).astype(F32)
    here = spread(place) == which
    pick_ref[...] = jnp.where(here, 1.0, 0.0).astype(BF16)
    halves(jnp.where(here, spread(weight), 0.0).T, share_ref)
    last = place == float(ROWS)
    nine_ref[...] = jnp.where(last, 1.0, 0.0).astype(BF16)
    halves(jnp.where(last, weight, 0.0).T, ninth_ref)


def project_kernel(parts, shared, *refs):
    pieces = refs[: parts - 1]
    part_ref, w_ref, gain_ref, pick_ref, nine_ref, hidden_ref, o_ref, normed_s, fold_s = refs[parts - 1 :]
    power = jnp.zeros((TOK, 1), F32)
    step = 512
    for c in range(0, D, step):
        h = part_ref[:, c : c + step]
        for s in range(1, parts):
            h += dot(head_rows(pieces[s - 1], shared), w_ref[weight_rows(parts, shared, s), c : c + step])
        hidden_ref[:, c : c + step] = h
        power += jnp.sum(h * h, axis=-1, keepdims=True)
    scale = lax.rsqrt(power * (1.0 / D) + 1e-06)
    for c in range(0, D, step):
        normed_s[:, c : c + step] = (
            hidden_ref[:, c : c + step] * scale * gain_ref[:, c : c + step]
        ).astype(BF16)
    for c in range(ROWS):
        piece = normed_s[:, c * FOLD : (c + 1) * FOLD]
        o_ref[:, c * FOLD : (c + 1) * FOLD] = dot(pick_ref[...], piece).astype(BF16)
        put_fold(fold_s, c, dot(nine_ref[...], piece))
    o_ref[:, D:] = whole_fold(fold_s)


def expert_kernel(count, x_ref, wide_ref, down_ref, o_ref, last_s, fold_s):
    def mlp(x):
        gate = dot(x, wide_ref[:, :FF])
        up = dot(x, wide_ref[:, FF:])
        inner = (gate / (1.0 + jnp.exp(-gate)) * up).astype(BF16)
        return dot(inner, down_ref[...])

    block = 256
    for b in range(0, count * ROWS, block):
        o_ref[b : b + block, :D] = mlp(x_ref[b : b + block, :D]).astype(BF16)
    load_fold(fold_s, x_ref[:, D:])
    for c in range(ROWS):
        last_s[:, c * FOLD : (c + 1) * FOLD] = take_fold(fold_s, c, count)
    last = mlp(last_s[...])
    for c in range(ROWS):
        put_fold(fold_s, c, last[:, c * FOLD : (c + 1) * FOLD])
    o_ref[:, D:] = whole_fold(fold_s)


def combine_kernel(y_ref, share_ref, ninth_ref, hidden_ref, o_ref, fold_s):
    load_fold(fold_s, y_ref[:, D:])
    for c in range(ROWS):
        cols = slice(c * FOLD, (c + 1) * FOLD)
        last = take_fold(fold_s, c, EXPERTS)
        mixture = dot(share_ref[...], y_ref[:, cols]) + dot(ninth_ref[...], last)
        o_ref[:, cols] = (hidden_ref[:, cols] + mixture[:TOK] + mixture[TOK:]).astype(BF16)


def exchange(value, axes):
    return lax.all_to_all(value, axes, split_axis=0, concat_axis=0, tiled=True)


def shaped(*dims, dtype=BF16):
    return jax.ShapeDtypeStruct(dims, dtype)


def on_device(
    queries, keys, values, route_ids, route_weights, out_weight, norm_gain, gate_up, down_weight
):
    heads, parts = queries.shape[2] // HEAD, keys.shape[2] // HEAD
    shared = heads // parts
    size = lax.axis_size("seq")
    ids = route_ids[0].T

    def ahead(value, s):
        return lax.ppermute(value, "seq", [(i, (i + s * parts) % size) for i in range(size)])

    def across(value, d):
        return lax.ppermute(value, "seq", [(i, i ^ d) for i in range(size)])

    kv, query = shaped(2 * TOK, HEAD), shaped(shared * TOK, HEAD)
    sent = call(
        functools.partial(pack_kernel, parts, shared),
        (kv,) * parts + (query,) * parts,
        [pltpu.VMEM(a.shape[1:], BF16) for a in (queries, keys, values)] + [pltpu.SemaphoreType.DMA((3,))],
        limit=107 << 19,
        in_specs=[pl.BlockSpec(memory_space=pltpu.HBM)] * 3,
    )(queries[0], keys[0], values[0])
    kvs = [sent[0]] + [ahead(sent[s], s) for s in range(1, parts)]
    asked = [sent[parts]] + [ahead(sent[parts + s], s) for s in range(1, parts)]
    line = call(functools.partial(join_kernel, parts), shaped(parts * 2 * TOK, HEAD))(*kvs)
    flipped = across(line, 2)
    gathered = [line, across(line, 1), flipped, across(flipped, 1)]
    *attended, weight = call(
        functools.partial(attention_kernel, parts, shared),
        (query,) * parts + (shaped(*out_weight.shape),),
        [pltpu.VMEM((size * TOK, HEAD), BF16)] * 2
        + [pltpu.VMEM((parts * shared * TOK, HEAD), BF16)] * 2
        + [pltpu.SemaphoreType.DMA],
        limit=40 << 20,
        in_specs=[VMEM] * (4 + parts) + [pl.BlockSpec(memory_space=pltpu.HBM)],
        out_specs=(VMEM,) * (parts + 1),
    )(*gathered, *asked, out_weight)
    answers = [ahead(attended[s], s) for s in range(1, parts)]
    part, pick, nine, share, ninth = call(
        functools.partial(prepare_kernel, parts, shared),
        (
            shaped(TOK, D, dtype=F32),
            shaped(EXPERTS * ROWS, TOK),
            shaped(EXPERTS, TOK),
            shaped(2 * TOK, EXPERTS * ROWS),
            shaped(2 * TOK, EXPERTS),
        ),
    )(attended[0], weight, ids, route_weights[0].T)
    hidden, outgoing = call(
        functools.partial(project_kernel, parts, shared),
        (shaped(TOK, D, dtype=F32), shaped(EXPERTS * ROWS, WIDE)),
        [pltpu.VMEM((TOK, D), BF16), pltpu.VMEM((FOLD // HEAD, EXPERTS * ROWS, HEAD), F32)],
    )(*answers, part, weight, norm_gain[None], pick, nine)
    arrived = exchange(outgoing, ("grp", "seq"))
    fold = pltpu.VMEM((FOLD // HEAD, EXPERTS * ROWS, HEAD), F32)
    result = call(
        functools.partial(expert_kernel, EXPERTS),
        shaped(EXPERTS * ROWS, WIDE),
        [pltpu.VMEM((EXPERTS, D), BF16), fold],
    )(arrived, gate_up[0], down_weight[0])
    returned = exchange(result, ("grp", "seq"))
    mixed = call(combine_kernel, shaped(TOK, D), [fold])(returned, share, ninth, hidden)
    return mixed[None]


def solution(mesh):
    placed = (
        P("grp", "seq", None),
        P("grp", "seq", None),
        P("grp", "seq", None),
        P("grp", "seq", None),
        P("grp", "seq", None),
        P(),
        P(),
        P(("grp", "seq"), None, None),
        P(("grp", "seq"), None, None),
    )

    return jax.shard_map(on_device, mesh=mesh, in_specs=placed, out_specs=P("grp", "seq", None), check_vma=False)
```

```python
import functools

import jax
import jax.numpy as jnp
from jax import lax
from jax.experimental import pallas as pl
from jax.experimental.pallas import tpu as pltpu
from jax.sharding import PartitionSpec as P


BF16, F32 = jnp.bfloat16, jnp.float32
D = 2048
HEAD = 128
FF = 768
TOP = 8
ROWS = 8
FOLD = D // ROWS
WIDE = D + FOLD
EXPERTS = 128
TOK = 128
VMEM = pl.BlockSpec(memory_space=pltpu.VMEM)


def dot(a, b, dims=((1,), (0,))):
    return lax.dot_general(a, b, (dims, ((), ())), preferred_element_type=F32)


def iota(shape, dim):
    return lax.broadcasted_iota(jnp.int32, shape, dim)


def call(kernel, out, scratch=(), limit=20 << 20, cost=None, **spec):
    return pl.pallas_call(
        kernel,
        out_shape=out,
        scratch_shapes=scratch,
        compiler_params=pltpu.CompilerParams(vmem_limit_bytes=limit),
        cost_estimate=cost,
        **spec,
    )


def pack_kernel(parts, shared, q_far, k_far, v_far, *refs):
    outs, (q_ref, k_ref, v_ref, sems) = refs[: 2 * parts], refs[2 * parts :]
    loads = [
        pltpu.make_async_copy(far, near, sems.at[n])
        for n, (far, near) in enumerate(((k_far, k_ref), (v_far, v_ref), (q_far, q_ref)))
    ]
    for load in loads:
        load.start()
    mine = lax.axis_index("seq") // parts
    for load in loads:
        load.wait()
    for s in range(parts):
        g = lax.rem(mine + s, parts)
        kv_ref, query_ref = outs[s], outs[parts + s]
        lane = pl.multiple_of(g * HEAD, HEAD)
        kv_ref[:TOK, :] = k_ref[:, pl.ds(lane, HEAD)]
        kv_ref[TOK:, :] = v_ref[:, pl.ds(lane, HEAD)]
        for h in range(shared):
            lane = pl.multiple_of(g * (shared * HEAD), HEAD) + h * HEAD
            query_ref[h * TOK : (h + 1) * TOK, :] = q_ref[:, pl.ds(lane, HEAD)]


def join_kernel(parts, *refs):
    mine = lax.axis_index("seq") // parts
    for s in range(parts):
        at = pl.multiple_of(lax.rem(mine - s + parts, parts) * (2 * TOK), 2 * TOK)
        refs[parts][pl.ds(at, 2 * TOK), :] = refs[s][...]


def attention_kernel(parts, shared, *refs):
    kvs, queries, w_ref = refs[:4], refs[4 : 4 + parts], refs[4 + parts]
    outs, near_ref = refs[5 + parts : 5 + 2 * parts], refs[5 + 2 * parts]
    k_s, v_s, q_s, o_s, sem = refs[6 + 2 * parts :]
    carry = pltpu.make_async_copy(w_ref, near_ref, sem)
    carry.start()
    me = lax.axis_index("seq")
    mine, lane_id = me // parts, lax.rem(me, parts)
    rows, keys = shared * TOK, 4 * TOK
    for d in range(4):
        for p in range(parts):
            at = pl.multiple_of((p * 4 + (lane_id ^ d)) * TOK, TOK)
            k_s[pl.ds(at, TOK), :] = kvs[d][p * 2 * TOK : (p * 2 + 1) * TOK, :]
            v_s[pl.ds(at, TOK), :] = kvs[d][(p * 2 + 1) * TOK : (p * 2 + 2) * TOK, :]
    for s in range(parts):
        at = pl.multiple_of(lax.rem(mine - s + parts, parts) * rows, rows)
        q_s[pl.ds(at, rows), :] = queries[s][...]
    factor = HEAD ** (-0.5) * 1.4426950408889634
    keep = iota((rows, keys), 1) <= iota((rows, keys), 0) % TOK + lane_id * TOK
    for i in range(parts):
        q = q_s[i * rows : (i + 1) * rows, :]
        own = dot(q, k_s[i * keys : (i + 1) * keys, :], ((1,), (1,)))
        own = jnp.where(keep, own, -jnp.inf)
        top = jnp.max(own, axis=-1, keepdims=True)
        if i:
            past = dot(q, k_s[: i * keys, :], ((1,), (1,)))
            top = jnp.maximum(top, jnp.max(past, axis=-1, keepdims=True))
            past = jnp.exp2((past - top) * factor)
        own = jnp.exp2((own - top) * factor)
        total = jnp.sum(own, axis=-1, keepdims=True)
        if i:
            total += jnp.sum(past, axis=-1, keepdims=True)
        share = 1.0 / total
        out = dot((own * share).astype(BF16), v_s[i * keys : (i + 1) * keys, :])
        if i:
            out += dot((past * share).astype(BF16), v_s[: i * keys, :])
        o_s[i * rows : (i + 1) * rows, :] = out.astype(BF16)
    for s in range(parts):
        at = pl.multiple_of(lax.rem(mine + s, parts) * rows, rows)
        outs[s][...] = o_s[pl.ds(at, rows), :]
    carry.wait()


def named(ids):
    experts = iota((EXPERTS, TOK), 0)
    return [ids[j : j + 1, :] == experts for j in range(TOP)]


def places(ids):
    hit = jnp.zeros((EXPERTS, TOK), F32)
    for match in named(ids):
        hit += jnp.where(match, 1.0, 0.0)
    before = jnp.where(iota((TOK, TOK), 0) < iota((TOK, TOK), 1), 1.0, 0.0).astype(BF16)
    return jnp.where(hit > 0.5, dot(hit.astype(BF16), before), -1.0)


def spread(rows):
    n, t = rows.shape
    return jnp.broadcast_to(rows[:, None, :], (n, ROWS, t)).reshape(n * ROWS, t)


def put_fold(fold_s, c, value):
    for half in range(FOLD // HEAD):
        fold_s[half, pl.ds(c, value.shape[0], stride=ROWS), :] = value[:, half * HEAD : (half + 1) * HEAD]


def take_fold(fold_s, c, count):
    halves = [fold_s[half, pl.ds(c, count, stride=ROWS), :] for half in range(FOLD // HEAD)]
    return jnp.concatenate(halves, axis=1).astype(BF16)


def load_fold(fold_s, tail):
    for half in range(FOLD // HEAD):
        fold_s[half] = tail[:, half * HEAD : (half + 1) * HEAD].astype(F32)


def whole_fold(fold_s):
    return jnp.concatenate([fold_s[half] for half in range(FOLD // HEAD)], axis=1).astype(BF16)


def head_rows(piece, shared):
    return jnp.concatenate([piece[g * TOK : (g + 1) * TOK, :] for g in range(shared)], axis=1)


def weight_rows(parts, shared, s):
    mine = lax.axis_index("seq") // parts
    wide = shared * HEAD
    return pl.ds(pl.multiple_of(lax.rem(mine - s + parts, parts) * wide, wide), wide)


def prepare_kernel(
    parts, shared, a_ref, w_ref, ids_ref, weights_ref, part_ref, pick_ref, nine_ref, share_ref, ninth_ref
):
    a = head_rows(a_ref, shared)
    rows = weight_rows(parts, shared, 0)
    for c in range(0, D, 512):
        part_ref[:, c : c + 512] = dot(a, w_ref[rows, c : c + 512])

    def halves(value, ref):
        high = value.astype(BF16)
        ref[:TOK, :] = high
        ref[TOK:, :] = (value - high.astype(F32)).astype(BF16)

    ids = ids_ref[...]
    place = places(ids)
    weight = jnp.zeros((EXPERTS, TOK), F32)
    for j, match in enumerate(named(ids)):
        weight += jnp.where(match, weights_ref[j : j + 1, :], 0.0)
    which = (iota((EXPERTS * ROWS, TOK), 0) % ROWS).astype(F32)
    here = spread(place) == which
    pick_ref[...] = jnp.where(here, 1.0, 0.0).astype(BF16)
    halves(jnp.where(here, spread(weight), 0.0).T, share_ref)
    last = place == float(ROWS)
    nine_ref[...] = jnp.where(last, 1.0, 0.0).astype(BF16)
    halves(jnp.where(last, weight, 0.0).T, ninth_ref)


def project_kernel(parts, shared, *refs):
    pieces = refs[: parts - 1]
    part_ref, w_ref, gain_ref, pick_ref, nine_ref, hidden_ref, o_ref, normed_s, fold_s = refs[parts - 1 :]
    power = jnp.zeros((TOK, 1), F32)
    step = 512
    for c in range(0, D, step):
        h = part_ref[:, c : c + step]
        for s in range(1, parts):
            h += dot(head_rows(pieces[s - 1], shared), w_ref[weight_rows(parts, shared, s), c : c + step])
        hidden_ref[:, c : c + step] = h
        power += jnp.sum(h * h, axis=-1, keepdims=True)
    scale = lax.rsqrt(power * (1.0 / D) + 1e-06)
    for c in range(0, D, step):
        normed_s[:, c : c + step] = (
            hidden_ref[:, c : c + step] * scale * gain_ref[:, c : c + step]
        ).astype(BF16)
    for c in range(ROWS):
        piece = normed_s[:, c * FOLD : (c + 1) * FOLD]
        o_ref[:, c * FOLD : (c + 1) * FOLD] = dot(pick_ref[...], piece).astype(BF16)
        put_fold(fold_s, c, dot(nine_ref[...], piece))
    o_ref[:, D:] = whole_fold(fold_s)


def expert_kernel(count, x_ref, wide_ref, down_ref, o_ref, last_s, fold_s):
    def mlp(x):
        gate = dot(x, wide_ref[:, :FF])
        up = dot(x, wide_ref[:, FF:])
        inner = (gate / (1.0 + jnp.exp(-gate)) * up).astype(BF16)
        return dot(inner, down_ref[...])

    block = 256
    for b in range(0, count * ROWS, block):
        o_ref[b : b + block, :D] = mlp(x_ref[b : b + block, :D]).astype(BF16)
    load_fold(fold_s, x_ref[:, D:])
    for c in range(ROWS):
        last_s[:, c * FOLD : (c + 1) * FOLD] = take_fold(fold_s, c, count)
    last = mlp(last_s[...])
    for c in range(ROWS):
        put_fold(fold_s, c, last[:, c * FOLD : (c + 1) * FOLD])
    o_ref[:, D:] = whole_fold(fold_s)


def combine_kernel(y_ref, share_ref, ninth_ref, hidden_ref, o_ref, fold_s):
    load_fold(fold_s, y_ref[:, D:])
    for c in range(ROWS):
        cols = slice(c * FOLD, (c + 1) * FOLD)
        last = take_fold(fold_s, c, EXPERTS)
        mixture = dot(share_ref[...], y_ref[:, cols]) + dot(ninth_ref[...], last)
        o_ref[:, cols] = (hidden_ref[:, cols] + mixture[:TOK] + mixture[TOK:]).astype(BF16)


def exchange(value, axes):
    return lax.all_to_all(value, axes, split_axis=0, concat_axis=0, tiled=True)


def shaped(*dims, dtype=BF16):
    return jax.ShapeDtypeStruct(dims, dtype)


def on_device(
    queries, keys, values, route_ids, route_weights, out_weight, norm_gain, gate_up, down_weight
):
    heads, parts = queries.shape[2] // HEAD, keys.shape[2] // HEAD
    shared = heads // parts
    size = lax.axis_size("seq")
    ids = route_ids[0].T

    def ahead(value, s):
        return lax.ppermute(value, "seq", [(i, (i + s * parts) % size) for i in range(size)])

    def across(value, d):
        return lax.ppermute(value, "seq", [(i, i ^ d) for i in range(size)])

    kv, query = shaped(2 * TOK, HEAD), shaped(shared * TOK, HEAD)
    sent = call(
        functools.partial(pack_kernel, parts, shared),
        (kv,) * parts + (query,) * parts,
        [pltpu.VMEM(a.shape[1:], BF16) for a in (queries, keys, values)] + [pltpu.SemaphoreType.DMA((3,))],
        limit=107 << 19,
        in_specs=[pl.BlockSpec(memory_space=pltpu.HBM)] * 3,
    )(queries[0], keys[0], values[0])
    kvs = [sent[0]] + [ahead(sent[s], s) for s in range(1, parts)]
    asked = [sent[parts]] + [ahead(sent[parts + s], s) for s in range(1, parts - 1)]
    line = call(functools.partial(join_kernel, parts), shaped(parts * 2 * TOK, HEAD))(*kvs)
    flipped = across(line, 2)
    asked.append(ahead(sent[2 * parts - 1], parts - 1))
    opposite = across(flipped, 1)
    gathered = [line, across(line, 1), flipped, opposite]
    *attended, weight = call(
        functools.partial(attention_kernel, parts, shared),
        (query,) * parts + (shaped(*out_weight.shape),),
        [pltpu.VMEM((size * TOK, HEAD), BF16)] * 2
        + [pltpu.VMEM((parts * shared * TOK, HEAD), BF16)] * 2
        + [pltpu.SemaphoreType.DMA],
        limit=40 << 20,
        in_specs=[VMEM] * (4 + parts) + [pl.BlockSpec(memory_space=pltpu.HBM)],
        out_specs=(VMEM,) * (parts + 1),
    )(*gathered, *asked, out_weight)
    answers = [ahead(attended[s], s) for s in range(1, parts)]
    part, pick, nine, share, ninth = call(
        functools.partial(prepare_kernel, parts, shared),
        (
            shaped(TOK, D, dtype=F32),
            shaped(EXPERTS * ROWS, TOK),
            shaped(EXPERTS, TOK),
            shaped(2 * TOK, EXPERTS * ROWS),
            shaped(2 * TOK, EXPERTS),
        ),
    )(attended[0], weight, ids, route_weights[0].T)
    hidden, outgoing = call(
        functools.partial(project_kernel, parts, shared),
        (shaped(TOK, D, dtype=F32), shaped(EXPERTS * ROWS, WIDE)),
        [pltpu.VMEM((TOK, D), BF16), pltpu.VMEM((FOLD // HEAD, EXPERTS * ROWS, HEAD), F32)],
    )(*answers, part, weight, norm_gain[None], pick, nine)
    arrived = exchange(outgoing, ("grp", "seq"))
    fold = pltpu.VMEM((FOLD // HEAD, EXPERTS * ROWS, HEAD), F32)
    result = call(
        functools.partial(expert_kernel, EXPERTS),
        shaped(EXPERTS * ROWS, WIDE),
        [pltpu.VMEM((EXPERTS, D), BF16), fold],
    )(arrived, gate_up[0], down_weight[0])
    returned = exchange(result, ("grp", "seq"))
    mixed = call(combine_kernel, shaped(TOK, D), [fold])(returned, share, ninth, hidden)
    return mixed[None]


def solution(mesh):
    placed = (
        P("grp", "seq", None),
        P("grp", "seq", None),
        P("grp", "seq", None),
        P("grp", "seq", None),
        P("grp", "seq", None),
        P(),
        P(),
        P(("grp", "seq"), None, None),
        P(("grp", "seq"), None, None),
    )

    return jax.shard_map(on_device, mesh=mesh, in_specs=placed, out_specs=P("grp", "seq", None), check_vma=False)
```
